32 devices in a mesh: section: 4 (over y, x), dp: 8 (over z, core).
Axes of the slice: x: 2, y: 2, z: 4, core: 2. Of those that a mesh axis runs over, the one named last changes fastest.
Arguments:
- latent: bfloat16 [2048, 1536], P('dp'), may hold values from -6 to 6
- target: bfloat16 [2048, 1536], P('dp'), may hold values from -6 to 6
- camera_of_token: int32 [2048], P('dp'), may hold values from 0 to 5
- timestep_indices: int32 [2], replicated, may hold values from 0 to 49
- camera_embedding_table: bfloat16 [6, 1536], replicated, may hold values from -3 to 3
- timestep_embedding_table: bfloat16 [50, 1536], replicated, may hold values from -2.5 to 2.5
- layer_norm_gain: float32 [4, 1536], P('section'), may hold values from 0.25 to 1.75
- frozen_weight: bfloat16 [4, 1536, 1536], P('section', 'dp'), may hold values from -0.15625 to 0.15625
- adapter_down_weight: bfloat16 [4, 64, 1536], P('section'), may hold values from -0.15625 to 0.15625
- adapter_up_weight: bfloat16 [4, 64, 1536], P('section'), may hold values from -0.75 to 0.75
Outputs:
- grad_down: float32 [4, 64, 1536], P('section', None, 'dp')
- grad_up: float32 [4, 64, 1536], P('section', None, 'dp')
The draws below stay inside these ranges and needn't reach their ends.
Inputs may be any that keep to these rules, and one draw needn't show every extreme that they name: `timestep_indices`: indices of rows of timestep_embedding_table.
All inputs are finite; a program needn't handle non-finite values.
Results may differ from the reference program's by a relative error of at most 0.024.
Values may be sent and summed in bfloat16 or wider, within the bound.
A program may use at most 64 MiB of HBM per device.

```python
import math
import jax
import jax.numpy as jnp
from jax import lax

HIDDEN_WIDTH = 1536
ADAPTER_RANK = 64
TOK_DEV = 256
VIEWS = 6
TSTEPS = 50
LAYER_COUNT = 4
TOKENS = 2048
N_DP = 8


def set_ends(values, stream_key, low, top_value):
    index_at = [jax.random.randint(jax.random.fold_in(stream_key, axis), (), 0, length) for axis, length in enumerate(values.shape)]
    longest = values.shape.index(max(values.shape))
    beside = index_at[:longest] + [(index_at[longest] + 1) % values.shape[longest]] + index_at[longest + 1:]
    return values.at[tuple(index_at)].set(low).at[tuple(beside)].set(top_value)


def with_spikes(drawn, own_key, source, target, shards_of, factor):
    owner, partner = [(jnp.arange(drawn.shape[axis_at]) // (drawn.shape[axis_at] // shards_of)).reshape([-1 if axis == axis_at else 1 for axis in range(drawn.ndim)]) for axis_at in (source, target)]
    chosen = jax.random.permutation(own_key, shards_of)[partner]
    strong = (owner == chosen) | (owner == (partner + shards_of // 2) % shards_of)
    return jnp.where(strong, factor * drawn, drawn)


def shard_levels(rng, extent, shards, smallest, largest):
    def one(position, parts):
        heights = jax.random.uniform(jax.random.fold_in(jax.random.fold_in(rng, 6), position), (parts,), jnp.float32, smallest / len(shards), largest / len(shards))
        return jnp.repeat(jnp.exp(heights), extent[position] // parts).reshape((-1,) + (1,) * (len(extent) - position - 1))

    factor_of = one(*shards[0])
    for cut in shards[1:]:
        factor_of = factor_of * one(*cut)
    return factor_of


def gaussian(own_key, dims, width, bound, cuts=(), kind=jnp.bfloat16):
    factor_of = shard_levels(own_key, dims, cuts, -0.22, 0.18) if cuts else 1.0
    values = jax.random.normal(own_key, dims, jnp.float32) * width * factor_of
    return jnp.minimum(jnp.maximum(values, -bound), bound).astype(kind)


def gaussian_with(rng, dims, scale, bound, shards, heavy, held_as=jnp.bfloat16):
    drawn = scale * jax.random.normal(rng, dims, jnp.float32)
    if shards:
        drawn = drawn * shard_levels(rng, dims, shards, -0.22, 0.18)
    return jnp.clip(with_spikes(drawn, jax.random.fold_in(rng, 3), *heavy), -bound, bound).astype(held_as)


def setup_inputs(seed: int = 0) -> dict:
    keys = jax.random.split(jax.random.key(seed), 11)
    return {
        "latent": gaussian(keys[0], (TOKENS, HIDDEN_WIDTH), 1.0, 6.0, ((0, 8),)),
        "target": gaussian_with(keys[1], (TOKENS, HIDDEN_WIDTH), 1.0, 6.0, ((0, 8),), (0, 1, 8, 2.0)),
        "camera_of_token": set_ends(jax.random.randint(keys[2], (TOKENS,), 0, VIEWS), jax.random.fold_in(keys[2], 1), 0, VIEWS - 1).astype(jnp.int32),
        "timestep_indices": jax.random.randint(keys[3], (2,), 0, TSTEPS).astype(jnp.int32),
        "camera_embedding_table": gaussian(keys[4], (VIEWS, HIDDEN_WIDTH), 0.5, 3.0),
        "timestep_embedding_table": gaussian(keys[5], (TSTEPS, HIDDEN_WIDTH), 0.3, 2.5),
        "layer_norm_gain": jnp.clip(1.0 + 0.15 * jax.random.normal(keys[6], (LAYER_COUNT, HIDDEN_WIDTH), jnp.float32), 0.25, 1.75),
        "frozen_weight": gaussian(keys[7], (LAYER_COUNT, HIDDEN_WIDTH, HIDDEN_WIDTH), HIDDEN_WIDTH ** -0.5, 0.15625, ((0, 4), (1, 8))),
        "adapter_down_weight": gaussian(keys[8], (LAYER_COUNT, ADAPTER_RANK, HIDDEN_WIDTH), HIDDEN_WIDTH ** -0.5, 0.15625, ((0, 4),)),
        "adapter_up_weight": gaussian(keys[9], (LAYER_COUNT, ADAPTER_RANK, HIDDEN_WIDTH), ADAPTER_RANK ** -0.5, 0.75, ((0, 4),)),
    }


BLEND = 0.5
ADAPTER_SCALE = 0.5
EPSILON = 1e-06

def forward_layer_pass(hidden_state, layer_weight, down_weight_rows, up_weight_rows, gain_row, modulate_row):
    hidden_float = hidden_state.astype(jnp.float32)
    inverse_rms = lax.rsqrt(lax.optimization_barrier(jnp.mean(hidden_float * hidden_float, axis=-1, keepdims=True)) + EPSILON)
    normalized_hidden = (hidden_float * inverse_rms * (gain_row * modulate_row)).astype(jnp.bfloat16)
    low_rank_hidden = lax.dot_general(normalized_hidden, down_weight_rows, (((1,), (1,)), ((), ())), preferred_element_type=jnp.float32).astype(jnp.bfloat16)
    preactivation = jnp.dot(normalized_hidden, layer_weight, preferred_element_type=jnp.float32) + ADAPTER_SCALE * jnp.dot(low_rank_hidden, up_weight_rows, preferred_element_type=jnp.float32)
    output = (hidden_float + jax.nn.silu(preactivation)).astype(jnp.bfloat16)
    return (output, normalized_hidden, low_rank_hidden, preactivation)

def backward_layer_pass(hidden_state, normalized_hidden, low_rank_hidden, preactivation, output_gradient, layer_weight, down_weight_rows, up_weight_rows, gain_row, modulate_row):
    sigmoid_value = jax.nn.sigmoid(preactivation)
    preactivation_gradient = (output_gradient * sigmoid_value * (1.0 + preactivation * (1.0 - sigmoid_value))).astype(jnp.bfloat16)
    low_rank_gradient = (ADAPTER_SCALE * lax.dot_general(preactivation_gradient, up_weight_rows, (((1,), (1,)), ((), ())), preferred_element_type=jnp.float32)).astype(jnp.bfloat16)
    norm_grad = lax.dot_general(preactivation_gradient, layer_weight, (((1,), (1,)), ((), ())), preferred_element_type=jnp.float32) + jnp.dot(low_rank_gradient, down_weight_rows, preferred_element_type=jnp.float32)
    up_gradient_term = ADAPTER_SCALE * lax.dot_general(low_rank_hidden, preactivation_gradient, (((0,), (0,)), ((), ())), preferred_element_type=jnp.float32)
    down_gradient_term = lax.dot_general(low_rank_gradient, normalized_hidden, (((0,), (0,)), ((), ())), preferred_element_type=jnp.float32)
    hidden_float = hidden_state.astype(jnp.float32)
    inverse_rms = lax.rsqrt(lax.optimization_barrier(jnp.mean(hidden_float * hidden_float, axis=-1, keepdims=True)) + EPSILON)
    scaled = hidden_float * inverse_rms
    scaled_grad = norm_grad * (gain_row * modulate_row)
    hidden_gradient = output_gradient + inverse_rms * (scaled_grad - scaled * lax.optimization_barrier(jnp.mean(scaled_grad * scaled, axis=-1, keepdims=True)))
    return (hidden_gradient, down_gradient_term, up_gradient_term)

def reference(latent, target, camera_of_token, timestep_indices, camera_embedding_table, timestep_embedding_table, layer_norm_gain, frozen_weight, adapter_down_weight, adapter_up_weight):
    timestep_modulation = 1.0 + jnp.dot(jax.nn.one_hot(timestep_indices, TSTEPS, dtype=jnp.bfloat16), timestep_embedding_table, preferred_element_type=jnp.float32)
    scale_factor = 1.0 / math.sqrt(TOKENS)

    def block_grads(totals, pieces):
        latent_rows, target_rows, camera_index = pieces
        camera_rows = jnp.dot(jax.nn.one_hot(camera_index, VIEWS, dtype=jnp.bfloat16), camera_embedding_table, preferred_element_type=jnp.float32)
        latent_now = latent_rows
        saved = []
        final_latent = latent_rows.astype(jnp.float32)
        for current_step in range(2):
            hidden_state = (latent_now.astype(jnp.float32) + camera_rows).astype(jnp.bfloat16)
            layer_inputs = []
            for current_layer in range(LAYER_COUNT):
                layer_inputs.append(hidden_state)
                hidden_state = forward_layer_pass(hidden_state, frozen_weight[current_layer], adapter_down_weight[current_layer], adapter_up_weight[current_layer], layer_norm_gain[current_layer], timestep_modulation[current_step])[0]
            saved.append(layer_inputs)
            blended = BLEND * (latent_now.astype(jnp.float32) + hidden_state.astype(jnp.float32))
            if current_step == 0:
                latent_now = blended.astype(jnp.bfloat16)
            else:
                final_latent = blended
        squashed = jnp.tanh(final_latent)
        adjoint = target_rows.astype(jnp.float32) * (1.0 - squashed * squashed) * scale_factor
        down_totals, up_totals = totals
        carried = jnp.zeros_like(adjoint)
        for current_step in (1, 0):
            if current_step == 1:
                output_gradient = BLEND * adjoint
            else:
                output_gradient = BLEND * (BLEND * adjoint + carried)
            for current_layer in reversed(range(LAYER_COUNT)):
                hidden_state = saved[current_step][current_layer]
                forward_pieces_saved = forward_layer_pass(hidden_state, frozen_weight[current_layer], adapter_down_weight[current_layer], adapter_up_weight[current_layer], layer_norm_gain[current_layer], timestep_modulation[current_step])
                hidden_gradient, down_gradient_term, up_gradient_term = backward_layer_pass(hidden_state, forward_pieces_saved[1], forward_pieces_saved[2], forward_pieces_saved[3], output_gradient, frozen_weight[current_layer], adapter_down_weight[current_layer], adapter_up_weight[current_layer], layer_norm_gain[current_layer], timestep_modulation[current_step])
                down_totals = down_totals.at[current_layer].add(down_gradient_term)
                up_totals = up_totals.at[current_layer].add(up_gradient_term)
                rounded = lax.optimization_barrier(hidden_gradient.astype(jnp.bfloat16))
                output_gradient = rounded.astype(jnp.float32)
            carried = output_gradient
        return ((down_totals, up_totals), jnp.zeros((), jnp.float32))
    zeros = jnp.zeros((LAYER_COUNT, ADAPTER_RANK, HIDDEN_WIDTH), jnp.float32)
    pieces = (latent.reshape(N_DP, TOK_DEV, HIDDEN_WIDTH), target.reshape(N_DP, TOK_DEV, HIDDEN_WIDTH), camera_of_token.reshape(N_DP, TOK_DEV))
    result = lax.scan(block_grads, (zeros, zeros), pieces)
    totals = result[0]
    return (totals[0], totals[1])
```

```python
import math

import jax
import jax.numpy as jnp
from jax import lax
from jax.sharding import PartitionSpec as P

BLEND = 0.5
ADAPTER_SCALE = 0.5
EPSILON = 1e-06


def forward_layer_pass(
    hidden_state, layer_weight, down_weight_rows, up_weight_rows, gain_row, modulate_row
):
    hidden_float = hidden_state.astype(jnp.float32)
    inverse_rms = lax.rsqrt(jnp.mean(hidden_float * hidden_float, axis=-1, keepdims=True) + EPSILON)
    normalized_hidden = (hidden_float * inverse_rms * (gain_row * modulate_row)).astype(
        jnp.bfloat16
    )
    low_rank_hidden = lax.dot_general(
        normalized_hidden,
        down_weight_rows,
        (((1,), (1,)), ((), ())),
        preferred_element_type=jnp.float32,
    ).astype(jnp.bfloat16)
    preactivation = jnp.dot(
        normalized_hidden, layer_weight, preferred_element_type=jnp.float32
    ) + ADAPTER_SCALE * jnp.dot(low_rank_hidden, up_weight_rows, preferred_element_type=jnp.float32)
    output = (hidden_float + jax.nn.silu(preactivation)).astype(jnp.bfloat16)
    return (output, normalized_hidden, low_rank_hidden, preactivation)


def backward_layer_pass(
    hidden_state,
    normalized_hidden,
    low_rank_hidden,
    preactivation,
    output_gradient,
    layer_weight,
    down_weight_rows,
    up_weight_rows,
    gain_row,
    modulate_row,
):
    sigmoid_value = jax.nn.sigmoid(preactivation)
    preactivation_gradient = (
        output_gradient * sigmoid_value * (1.0 + preactivation * (1.0 - sigmoid_value))
    ).astype(jnp.bfloat16)
    low_rank_gradient = (
        ADAPTER_SCALE
        * lax.dot_general(
            preactivation_gradient,
            up_weight_rows,
            (((1,), (1,)), ((), ())),
            preferred_element_type=jnp.float32,
        )
    ).astype(jnp.bfloat16)
    norm_grad = lax.dot_general(
        preactivation_gradient,
        layer_weight,
        (((1,), (1,)), ((), ())),
        preferred_element_type=jnp.float32,
    ) + jnp.dot(low_rank_gradient, down_weight_rows, preferred_element_type=jnp.float32)
    up_gradient_term = ADAPTER_SCALE * lax.dot_general(
        low_rank_hidden,
        preactivation_gradient,
        (((0,), (0,)), ((), ())),
        preferred_element_type=jnp.float32,
    )
    down_gradient_term = lax.dot_general(
        low_rank_gradient,
        normalized_hidden,
        (((0,), (0,)), ((), ())),
        preferred_element_type=jnp.float32,
    )
    hidden_float = hidden_state.astype(jnp.float32)
    inverse_rms = lax.rsqrt(jnp.mean(hidden_float * hidden_float, axis=-1, keepdims=True) + EPSILON)
    scaled = hidden_float * inverse_rms
    scaled_grad = norm_grad * (gain_row * modulate_row)
    hidden_gradient = output_gradient + inverse_rms * (
        scaled_grad - scaled * jnp.mean(scaled_grad * scaled, axis=-1, keepdims=True)
    )
    return (hidden_gradient, down_gradient_term, up_gradient_term)


def local(
    latent,
    target,
    camera_of_token,
    timestep_indices,
    camera_embedding_table,
    timestep_embedding_table,
    layer_norm_gain,
    frozen_weight,
    adapter_down_weight,
    adapter_up_weight,
):
    sections = lax.axis_size("section")
    ways = lax.axis_size("dp")
    position = lax.axis_index("section")
    width = latent.shape[1]
    rank = adapter_down_weight.shape[1]
    rows = latent.shape[0] // sections
    scale_factor = 1.0 / math.sqrt(latent.shape[0] * ways)
    weights = lax.all_gather(
        frozen_weight[0], ("section", "dp"), axis=0, tiled=True
    ).reshape(sections, width, width)
    adapters = lax.all_gather(
        jnp.concatenate([adapter_down_weight, adapter_up_weight], axis=1), "section", axis=0, tiled=True
    )
    down, up = adapters[:, :rank], adapters[:, rank:]
    gains = lax.all_gather(layer_norm_gain, "section", axis=0, tiled=True)
    mine = lambda array: lax.dynamic_slice_in_dim(array, position * rows, rows, 0)
    latent, target, camera_of_token = mine(latent), mine(target), mine(camera_of_token)
    camera_rows = jnp.dot(
        jax.nn.one_hot(camera_of_token, camera_embedding_table.shape[0], dtype=jnp.bfloat16),
        camera_embedding_table,
        preferred_element_type=jnp.float32,
    )
    modulation = 1.0 + jnp.dot(
        jax.nn.one_hot(timestep_indices, timestep_embedding_table.shape[0], dtype=jnp.bfloat16),
        timestep_embedding_table,
        preferred_element_type=jnp.float32,
    )
    saved = {}
    current = latent
    for step in range(2):
        hidden = (current.astype(jnp.float32) + camera_rows).astype(jnp.bfloat16)
        for layer in range(sections):
            output, *rest = forward_layer_pass(
                hidden, weights[layer], down[layer], up[layer], gains[layer], modulation[step]
            )
            saved[step, layer] = (hidden, *rest)
            hidden = output
        final = BLEND * (current.astype(jnp.float32) + hidden.astype(jnp.float32))
        current = final.astype(jnp.bfloat16)
    squashed = jnp.tanh(final)
    adjoint = target.astype(jnp.float32) * (1.0 - squashed * squashed) * scale_factor
    down_sum, up_sum = [0.0] * sections, [0.0] * sections
    cotangent = BLEND * adjoint
    for step in (1, 0):
        for layer in reversed(range(sections)):
            gradient, down_term, up_term = backward_layer_pass(
                *saved[step, layer],
                cotangent,
                weights[layer],
                down[layer],
                up[layer],
                gains[layer],
                modulation[step],
            )
            down_sum[layer] = down_sum[layer] + down_term
            up_sum[layer] = up_sum[layer] + up_term
            cotangent = gradient.astype(jnp.bfloat16).astype(jnp.float32)
        cotangent = BLEND * (BLEND * adjoint + cotangent)
    sums = jnp.concatenate([jnp.stack(down_sum), jnp.stack(up_sum)], axis=1)
    sums = sums.reshape(sections, 2 * rank, ways, width // ways).transpose(0, 2, 1, 3)
    sums = sums.reshape(sections * ways, 2 * rank, width // ways)
    part = lax.psum_scatter(sums, ("section", "dp"), scatter_dimension=0, tiled=True)
    return (part[:, :rank], part[:, rank:])


def solution(mesh):
    in_specs = (
        P("dp", None),
        P("dp", None),
        P("dp"),
        P(),
        P(),
        P(),
        P("section", None),
        P("section", "dp", None),
        P("section", None, None),
        P("section", None, None),
    )
    out_specs = (P("section", None, "dp"), P("section", None, "dp"))
    return jax.shard_map(local, mesh=mesh, in_specs=in_specs, out_specs=out_specs, check_vma=False)
```

```python
import functools
import math

import jax
import jax.numpy as jnp
from jax import lax
from jax.experimental import pallas as pl
from jax.experimental.pallas import tpu as pltpu
from jax.sharding import PartitionSpec as P

BLEND = 0.5
ADAPTER_SCALE = 0.5
EPSILON = 1e-06
MESH = pl.DeviceIdType.MESH
NT = (((1,), (1,)), ((), ()))
TN = (((0,), (0,)), ((), ()))


def bits_of(size):
    bits = size.bit_length() - 1
    return bits if 2**bits == size else 0


def section_at(place, size):
    bits = bits_of(size)
    if not bits:
        return place
    bit = [(place // 2**i) % 2 for i in range(bits)] + [0]
    return sum(((bit[i] + bit[i + 1]) % 2) * 2**i for i in range(bits))


def place_of(section, size):
    bits = bits_of(size)
    if not bits:
        return section
    upper, place = 0, 0
    for i in reversed(range(bits)):
        upper = ((section // 2**i) % 2 + upper) % 2
        place = place + upper * 2**i
    return place


def arrivals(size):
    half = size // 2
    steps = []
    for distance in range(1, half + 1):
        for way in (1, -1):
            if distance < half or size % 2:
                steps.append((way, distance, None))
            else:
                steps.append((way, distance, 0 if way == 1 else 1))
    return steps


def part_at(distance, way, size):
    if distance < size // 2 or size % 2:
        return None
    return 0 if way == 1 else 1


def kernel(
    sections,
    ways,
    scale_factor,
    steps_ref,
    latent_ref,
    target_ref,
    camera_ref,
    camera_table_ref,
    step_table_ref,
    gain_ref,
    shard_ref,
    down_ref,
    up_ref,
    out_ref,
    weights,
    adapters,
    gains,
    hidden_at,
    pre_at,
    low_at,
    modulation,
    camera_rows,
    adjoint_at,
    pair_out,
    pair_in,
    depth_out,
    depth_in,
    plane_out,
    plane_in,
    local_sem,
    first_send,
    first_recv,
    second_send,
    second_recv,
    twin_send,
    twin_recv,
    small_send,
    small_recv,
    adapter_send,
    adapter_recv,
    pair_sems,
    depth_send,
    depth_recv,
    plane_send,
    plane_recv,
):
    section, lane = lax.axis_index("section"), lax.axis_index("dp")
    depth_size = ways // 2
    depth, core = lane // 2, lane % 2
    place = place_of(section, sections)
    block, width = shard_ref.shape
    rows = hidden_at.shape[2]
    rank = down_ref.shape[0]
    twin = (section, depth * 2 + 1 - core)

    def on_section(other):
        return (other, lane)

    def on_depth(other):
        return (section, other * 2 + core)

    barrier = pltpu.get_barrier_semaphore()
    friends = [twin]
    friends += [on_section((section + k) % sections) for k in range(1, sections)]
    friends += [on_depth((depth + k) % depth_size) for k in range(1, depth_size)]
    for friend in friends:
        pl.semaphore_signal(barrier, inc=1, device_id=friend, device_id_type=MESH)
    pl.semaphore_wait(barrier, len(friends))

    def remote(source, target, send, recv, device):
        return pltpu.make_async_remote_copy(
            src_ref=source,
            dst_ref=target,
            send_sem=send,
            recv_sem=recv,
            device_id=device,
            device_id_type=MESH,
        )

    pending = []

    def go(copy):
        copy.start()
        pending.append(copy)

    go_gain, go_adapter = [], []
    for k in range(1, sections):
        other = on_section((section + k) % sections)
        copy = remote(gain_ref, gains.at[section], small_send.at[k], small_recv.at[k], other)
        copy.start()
        go_gain.append((copy, k))

    def region(home, row, half, part):
        columns = width // 2
        start = half * columns
        if part is not None:
            columns = columns // 2
            start = start + part * columns
        offset = pl.multiple_of((row * 2 + core) * block, block)
        return weights.at[home, pl.ds(offset, block), pl.ds(start, columns)]

    def own(half, part):
        columns = width // 2
        start = half * columns
        if part is not None:
            columns = columns // 2
            start = start + part * columns
        return shard_ref.at[:, pl.ds(start, columns)]

    local = [
        pltpu.make_async_copy(
            shard_ref,
            weights.at[section, pl.ds(pl.multiple_of(lane * block, block), block), :],
            local_sem.at[0],
        ),
        pltpu.make_async_copy(gain_ref, gains.at[section], local_sem.at[1]),
        pltpu.make_async_copy(down_ref, adapters.at[section, 0], local_sem.at[2]),
        pltpu.make_async_copy(up_ref, adapters.at[section, 1], local_sem.at[3]),
    ]
    for copy in local:
        copy.start()

    sizes = ((sections, depth_size), (depth_size, sections))
    spots = ((place, depth), (depth, place))

    def item(half, first, second):
        at_first = (spots[half][0] - first) % sizes[half][0]
        at_second = (spots[half][1] - second) % sizes[half][1]
        if half == 0:
            return section_at(at_first, sections), at_second
        return section_at(at_second, sections), at_first

    def neighbour(half, ring, way):
        if (half + ring) % 2 == 0:
            return on_section(section_at((place + way) % sections, sections))
        return on_depth((depth + way) % depth_size)

    def send(half, ring, first, second, way, distance):
        part = part_at(distance, way, sizes[half][ring])
        home, row = item(half, first, second)
        place_in = region(home, row, half, part)
        source = own(half, part) if first == 0 and second == 0 else place_in
        at = 0 if way == 1 else 1
        if ring == 0:
            sems = (first_send.at[half, at, distance], first_recv.at[half, at, distance])
        else:
            index = (half, first % sizes[half][0], at, distance)
            sems = (second_send.at[index], second_recv.at[index])
        go(remote(source, place_in, *sems, neighbour(half, ring, way)))

    def receive(half, ring, first, second, way, distance):
        part = part_at(distance, way, sizes[half][ring])
        home, row = item(half, first, second)
        place_in = region(home, row, half, part)
        at = 0 if way == 1 else 1
        if ring == 0:
            sems = (first_send.at[half, at, distance], first_recv.at[half, at, distance])
        else:
            index = (half, first % sizes[half][0], at, distance)
            sems = (second_send.at[index], second_recv.at[index])
        remote(place_in, place_in, *sems, neighbour(half, ring, way)).wait_recv()

    twins = []

    def share(half, first, second):
        home, row = item(half, first, second)
        place_in = region(home, row, half, None)
        source = own(half, None) if first == 0 and second == 0 else place_in
        index = (half, first % sizes[half][0], second % sizes[half][1])
        go(remote(source, place_in, twin_send.at[index], twin_recv.at[index], twin))
        twins.append((half, first, second, index))

    def whole(half, first, second):
        if second == 0:
            for way in (1, -1):
                send(half, 1, first, 0, way, 1)
        share(half, first, second)

    def on_first(half, way, distance):
        size = sizes[half][0]
        receive(half, 0, way * distance, 0, way, distance)
        if (distance + 1) * 2 <= size:
            send(half, 0, way * distance, 0, way, distance + 1)
        if part_at(distance, way, size) is None or way == -1:
            whole(half, way * distance, 0)

    def on_second(half, first, way, distance):
        size = sizes[half][1]
        receive(half, 1, first, way * distance, way, distance)
        if (distance + 1) * 2 <= size:
            send(half, 1, first, way * distance, way, distance + 1)
        if part_at(distance, way, size) is None or way == -1:
            whole(half, first, way * distance)

    events = []
    for half in (0, 1):
        for way, distance, _ in arrivals(sizes[half][0]):
            events.append((distance, 0, half, 0, 0, way, distance))
        firsts = [(0, 0)]
        for way, distance, part in arrivals(sizes[half][0]):
            if part is None or way == -1:
                firsts.append((way * distance, distance))
        for first, ready in firsts:
            for way, distance, _ in arrivals(sizes[half][1]):
                events.append((ready + distance, 1, half, ready, first, way, distance))
    events.sort(key=lambda event: (event[0], event[1], event[3], event[6]))

    for half in (0, 1):
        for way in (1, -1):
            send(half, 0, 0, 0, way, 1)
    for half in (0, 1):
        whole(half, 0, 0)
    for k in range(1, sections):
        other = on_section((section + k) % sections)

        @pl.when(core == 0)
        def _():
            remote(
                down_ref, adapters.at[section, 0], adapter_send.at[k], adapter_recv.at[k], other
            ).start()

        @pl.when(core == 1)
        def _():
            remote(
                up_ref, adapters.at[section, 1], adapter_send.at[k], adapter_recv.at[k], other
            ).start()

    mine = pl.ds(pl.multiple_of(section * rows, rows), rows)
    cameras = camera_ref[mine, :]
    table = camera_table_ref[...].astype(jnp.float32)
    chosen = jnp.zeros((rows, width), jnp.float32)
    for view in range(table.shape[0]):
        chosen = jnp.where(cameras == view, table[view : view + 1, :], chosen)
    camera_rows[...] = chosen
    latent = latent_ref[mine, :].astype(jnp.float32)
    hidden_at[0, 0] = (latent + chosen).astype(jnp.bfloat16)
    step_table = step_table_ref[...].astype(jnp.float32)
    step_rows = lax.broadcasted_iota(jnp.int32, step_table.shape, 0)
    for step in range(2):
        picked = jnp.where(step_rows == steps_ref[step], step_table, 0.0)
        modulation[step] = 1.0 + jnp.sum(picked, axis=0, keepdims=True)

    for _, ring, half, _, first, way, distance in events:
        if ring == 0:
            on_first(half, way, distance)
        else:
            on_second(half, first, way, distance)

    for k in range(1, sections):
        behind = (section - k) % sections
        held = adapters.at[behind, core]
        remote(held, held, adapter_send.at[k], adapter_recv.at[k], on_section(behind)).wait()
        go(remote(held, held, adapter_send.at[sections + k], adapter_recv.at[sections + k], twin))
    for k in range(1, sections):
        behind = (section - k) % sections
        held = adapters.at[behind, 1 - core]
        index = sections + k
        remote(held, held, adapter_send.at[index], adapter_recv.at[index], twin).wait_recv()
    for copy, k in go_gain:
        copy.wait()
    for half, first, second, index in twins:
        home, row = item(half, first, second)
        columns = width // 2
        offset = pl.multiple_of((row * 2 + 1 - core) * block, block)
        held = weights.at[home, pl.ds(offset, block), pl.ds(half * columns, columns)]
        remote(held, held, twin_send.at[index], twin_recv.at[index], twin).wait_recv()
    for copy in local:
        copy.wait()
    for copy in pending:
        copy.wait_send()
    pending.clear()

    def normed_of(step, layer):
        hidden = hidden_at[step, layer].astype(jnp.float32)
        inverse = lax.rsqrt(jnp.mean(hidden * hidden, axis=-1, keepdims=True) + EPSILON)
        gain = gains[layer] * modulation[step]
        return hidden, inverse, gain, (hidden * inverse * gain).astype(jnp.bfloat16)

    def forward(step, layer):
        hidden, _, _, normed = normed_of(step, layer)
        low = lax.dot_general(
            normed, adapters[layer, 0], NT, preferred_element_type=jnp.float32
        ).astype(jnp.bfloat16)
        pre = jnp.dot(
            normed, weights[layer], preferred_element_type=jnp.float32
        ) + ADAPTER_SCALE * jnp.dot(low, adapters[layer, 1], preferred_element_type=jnp.float32)
        pre_at[step, layer] = pre
        low_at[step, layer] = low
        hidden_at[step, layer + 1] = (hidden + jax.nn.silu(pre)).astype(jnp.bfloat16)

    def forward_body(index, carry):
        step, layer = index // sections, index % sections
        forward(step, layer)

        @pl.when((step == 0) & (layer == sections - 1))
        def _():
            last = hidden_at[0, sections].astype(jnp.float32)
            first = latent_ref[mine, :].astype(jnp.float32)
            middle = (BLEND * (first + last)).astype(jnp.bfloat16)
            hidden_at[0, sections] = middle
            hidden_at[1, 0] = (middle.astype(jnp.float32) + camera_rows[...]).astype(jnp.bfloat16)

        return carry

    lax.fori_loop(0, 2 * sections, forward_body, 0)
    final = BLEND * (
        hidden_at[0, sections].astype(jnp.float32) + hidden_at[1, sections].astype(jnp.float32)
    )
    squashed = jnp.tanh(final)
    adjoint = (
        target_ref[mine, :].astype(jnp.float32) * (1.0 - squashed * squashed) * scale_factor
    )
    adjoint_at[...] = adjoint

    def backward(step, layer, gradient, earlier):
        hidden, inverse, gain, normed = normed_of(step, layer)
        pre = pre_at[step, layer]
        sigmoid = jax.nn.sigmoid(pre)
        pre_grad = (gradient * sigmoid * (1.0 + pre * (1.0 - sigmoid))).astype(jnp.bfloat16)
        low_grad = (
            ADAPTER_SCALE
            * lax.dot_general(
                pre_grad, adapters[layer, 1], NT, preferred_element_type=jnp.float32
            )
        ).astype(jnp.bfloat16)
        norm_grad = lax.dot_general(
            pre_grad, weights[layer], NT, preferred_element_type=jnp.float32
        ) + jnp.dot(low_grad, adapters[layer, 0], preferred_element_type=jnp.float32)
        down_term = lax.dot_general(normed, low_grad, TN, preferred_element_type=jnp.float32)
        up_term = ADAPTER_SCALE * lax.dot_general(
            pre_grad, low_at[step, layer], TN, preferred_element_type=jnp.float32
        )
        terms = jnp.concatenate([down_term, up_term], axis=1)
        terms = terms.reshape(depth_size, 2, block, 2 * rank)
        for side in range(2):
            total = terms[:, side]
            if earlier:
                total = total + pair_out[layer, side].astype(jnp.float32)
            pair_out[layer, side] = total.astype(jnp.bfloat16)
        scaled = hidden * inverse
        scaled_grad = norm_grad * gain
        result = gradient + inverse * (
            scaled_grad - scaled * jnp.mean(scaled_grad * scaled, axis=-1, keepdims=True)
        )
        return result.astype(jnp.bfloat16).astype(jnp.float32)

    def to_twin(layer):
        return remote(
            pair_out.at[layer, 1 - core],
            pair_in.at[layer],
            pair_sems.at[0, layer],
            pair_sems.at[1, layer],
            twin,
        )

    def to_depth(layer, k):
        other = (depth + k) % depth_size
        return remote(
            depth_out.at[layer, other],
            depth_in.at[layer, k - 1],
            depth_send.at[layer, k],
            depth_recv.at[layer, k],
            on_depth(other),
        )

    def pass_on(layer):
        to_twin(layer).wait_recv()
        total = pair_out[layer, core].astype(jnp.float32) + pair_in[layer].astype(jnp.float32)
        depth_out[layer] = total.astype(jnp.bfloat16)
        for k in range(1, depth_size):
            to_depth(layer, k).start()

    def late_body(index, gradient):
        layer = sections - 1 - index
        gradient = backward(1, layer, gradient, False)
        return gradient

    def early_body(index, gradient):
        layer = sections - 1 - index
        gradient = backward(0, layer, gradient, True)
        to_twin(layer).start()

        @pl.when(index > 0)
        def _():
            pass_on(layer + 1)

        return gradient

    gradient = lax.fori_loop(0, sections, late_body, BLEND * adjoint)
    gradient = BLEND * (BLEND * adjoint_at[...] + gradient)
    lax.fori_loop(0, sections, early_body, gradient)
    pass_on(0)

    def settle(layer, carry):
        total = depth_out[layer, depth].astype(jnp.float32)
        for k in range(1, depth_size):
            to_depth(layer, k).wait()
            total = total + depth_in[layer, k - 1].astype(jnp.float32)
        plane_out[layer] = total.astype(jnp.bfloat16)
        to_twin(layer).wait_send()
        return carry

    lax.fori_loop(0, sections, settle, 0)
    copies = []
    for k in range(1, sections):
        other = (section + k) % sections
        copy = remote(
            plane_out.at[other],
            plane_in.at[k - 1],
            plane_send.at[k],
            plane_recv.at[k],
            on_section(other),
        )
        copy.start()
        copies.append(copy)
    total = plane_out[section].astype(jnp.float32)
    for k, copy in enumerate(copies):
        copy.wait()
        total = total + plane_in[k].astype(jnp.float32)
    out_ref[...] = total


def local(
    latent,
    target,
    camera_of_token,
    timestep_indices,
    camera_embedding_table,
    timestep_embedding_table,
    layer_norm_gain,
    frozen_weight,
    adapter_down_weight,
    adapter_up_weight,
):
    sections, ways = lax.axis_size("section"), lax.axis_size("dp")
    width = latent.shape[1]
    rank = adapter_down_weight.shape[1]
    block = frozen_weight.shape[1]
    rows = latent.shape[0] // sections
    depth_size = ways // 2
    scale_factor = 1.0 / math.sqrt(latent.shape[0] * ways)
    longest = max(sections, depth_size)
    dma = pltpu.SemaphoreType.DMA
    bf16, f32 = jnp.bfloat16, jnp.float32
    vmem = pl.BlockSpec(memory_space=pltpu.VMEM)
    result = pl.pallas_call(
        functools.partial(kernel, sections, ways, scale_factor),
        out_shape=jax.ShapeDtypeStruct((block, 2 * rank), f32),
        in_specs=[pl.BlockSpec(memory_space=pltpu.SMEM)] + [vmem] * 9,
        out_specs=vmem,
        scratch_shapes=[
            pltpu.VMEM((sections, width, width), bf16),
            pltpu.VMEM((sections, 2, rank, width), bf16),
            pltpu.VMEM((sections, 1, width), f32),
            pltpu.VMEM((2, sections + 1, rows, width), bf16),
            pltpu.VMEM((2, sections, rows, width), f32),
            pltpu.VMEM((2, sections, rows, rank), bf16),
            pltpu.VMEM((2, 1, width), f32),
            pltpu.VMEM((rows, width), f32),
            pltpu.VMEM((rows, width), f32),
            pltpu.VMEM((sections, 2, depth_size, block, 2 * rank), bf16),
            pltpu.VMEM((sections, depth_size, block, 2 * rank), bf16),
            pltpu.VMEM((sections, depth_size, block, 2 * rank), bf16),
            pltpu.VMEM((sections, depth_size - 1, block, 2 * rank), bf16),
            pltpu.VMEM((sections, block, 2 * rank), bf16),
            pltpu.VMEM((sections - 1, block, 2 * rank), bf16),
            dma((4,)),
            dma((2, 2, longest // 2 + 1)),
            dma((2, 2, longest // 2 + 1)),
            dma((2, longest, 2, longest // 2 + 1)),
            dma((2, longest, 2, longest // 2 + 1)),
            dma((2, longest, longest)),
            dma((2, longest, longest)),
            dma((sections,)),
            dma((sections,)),
            dma((2 * sections,)),
            dma((2 * sections,)),
            dma((2, sections)),
            dma((sections, depth_size)),
            dma((sections, depth_size)),
            dma((sections,)),
            dma((sections,)),
        ],
        compiler_params=pltpu.CompilerParams(
            collective_id=0, has_side_effects=True, vmem_limit_bytes=66 * 1024 * 1024 - 2 * 1024 * 1024 - 65536
        ),
    )(
        timestep_indices,
        latent,
        target,
        camera_of_token[:, None],
        camera_embedding_table,
        timestep_embedding_table,
        layer_norm_gain,
        frozen_weight[0],
        adapter_down_weight[0],
        adapter_up_weight[0],
    )
    turned = result.T
    return (turned[None, :rank], turned[None, rank:])


def solution(mesh):
    in_specs = (
        P("dp", None),
        P("dp", None),
        P("dp"),
        P(),
        P(),
        P(),
        P("section", None),
        P("section", "dp", None),
        P("section", None, None),
        P("section", None, None),
    )
    out_specs = (P("section", None, "dp"), P("section", None, "dp"))
    return jax.shard_map(local, mesh=mesh, in_specs=in_specs, out_specs=out_specs, check_vma=False)
```

```python
import functools
import math

import jax
import jax.numpy as jnp
from jax import lax
from jax.experimental import pallas as pl
from jax.experimental.pallas import tpu as pltpu
from jax.sharding import PartitionSpec as P

BLEND = 0.5
ADAPTER_SCALE = 0.5
EPSILON = 1e-06
MESH = pl.DeviceIdType.MESH
NT = (((1,), (1,)), ((), ()))
TN = (((0,), (0,)), ((), ()))


def bits_of(size):
    bits = size.bit_length() - 1
    return bits if 2**bits == size else 0


def section_at(place, size):
    bits = bits_of(size)
    if not bits:
        return place
    bit = [(place // 2**i) % 2 for i in range(bits)] + [0]
    return sum(((bit[i] + bit[i + 1]) % 2) * 2**i for i in range(bits))


def place_of(section, size):
    bits = bits_of(size)
    if not bits:
        return section
    upper, place = 0, 0
    for i in reversed(range(bits)):
        upper = ((section // 2**i) % 2 + upper) % 2
        place = place + upper * 2**i
    return place


def arrivals(size):
    half = size // 2
    steps = []
    for distance in range(1, half + 1):
        for way in (1, -1):
            if distance < half or size % 2:
                steps.append((way, distance, None))
            else:
                steps.append((way, distance, 0 if way == 1 else 1))
    return steps


def part_at(distance, way, size):
    if distance < size // 2 or size % 2:
        return None
    return 0 if way == 1 else 1


def kernel(
    sections,
    ways,
    scale_factor,
    steps_ref,
    latent_ref,
    target_ref,
    camera_ref,
    camera_table_ref,
    step_table_ref,
    gain_ref,
    shard_ref,
    down_ref,
    up_ref,
    out_ref,
    weights,
    adapters,
    gains,
    hidden_at,
    pre_at,
    low_at,
    modulation,
    camera_rows,
    adjoint_at,
    pair_out,
    pair_in,
    depth_out,
    depth_in,
    plane_out,
    plane_in,
    local_sem,
    first_send,
    first_recv,
    second_send,
    second_recv,
    twin_send,
    twin_recv,
    small_send,
    small_recv,
    adapter_send,
    adapter_recv,
    pair_sems,
    depth_send,
    depth_recv,
    plane_send,
    plane_recv,
):
    section, lane = lax.axis_index("section"), lax.axis_index("dp")
    depth_size = ways // 2
    depth, core = lane // 2, lane % 2
    place = place_of(section, sections)
    block, width = shard_ref.shape
    rows = hidden_at.shape[2]
    rank = down_ref.shape[0]
    twin = (section, depth * 2 + 1 - core)

    def on_section(other):
        return (other, lane)

    def on_depth(other):
        return (section, other * 2 + core)

    barrier = pltpu.get_barrier_semaphore()
    friends = [twin]
    friends += [on_section((section + k) % sections) for k in range(1, sections)]
    friends += [on_depth((depth + k) % depth_size) for k in range(1, depth_size)]
    for friend in friends:
        pl.semaphore_signal(barrier, inc=1, device_id=friend, device_id_type=MESH)
    pl.semaphore_wait(barrier, len(friends))

    def remote(source, target, send, recv, device):
        return pltpu.make_async_remote_copy(
            src_ref=source,
            dst_ref=target,
            send_sem=send,
            recv_sem=recv,
            device_id=device,
            device_id_type=MESH,
        )

    pending = []

    def go(copy):
        copy.start()
        pending.append(copy)

    go_gain, go_adapter = [], []
    for k in range(1, sections):
        other = on_section((section + k) % sections)
        copy = remote(gain_ref, gains.at[section], small_send.at[k], small_recv.at[k], other)
        copy.start()
        go_gain.append((copy, k))

    tiles = width // 128
    cut = max(tiles // 4, 1)

    def columns_of(half, part):
        start, stop = (0, cut) if half == 0 else (cut, tiles)
        middle = (start + stop) // 2
        if part is not None:
            start, stop = (start, middle) if part == 0 else (middle, stop)
        return pl.ds(start * 128, (stop - start) * 128)

    def region(home, row, half, part, side=core):
        offset = pl.multiple_of((row * 2 + side) * block, block)
        return weights.at[home, pl.ds(offset, block), columns_of(half, part)]

    def own(half, part):
        return shard_ref.at[:, columns_of(half, part)]

    local = [
        pltpu.make_async_copy(
            shard_ref,
            weights.at[section, pl.ds(pl.multiple_of(lane * block, block), block), :],
            local_sem.at[0],
        ),
        pltpu.make_async_copy(gain_ref, gains.at[section], local_sem.at[1]),
        pltpu.make_async_copy(down_ref, adapters.at[section, 0], local_sem.at[2]),
        pltpu.make_async_copy(up_ref, adapters.at[section, 1], local_sem.at[3]),
    ]
    for copy in local:
        copy.start()

    sizes = ((sections, depth_size), (depth_size, sections))
    spots = ((place, depth), (depth, place))

    def item(half, first, second):
        at_first = (spots[half][0] - first) % sizes[half][0]
        at_second = (spots[half][1] - second) % sizes[half][1]
        if half == 0:
            return section_at(at_first, sections), at_second
        return section_at(at_second, sections), at_first

    def neighbour(half, ring, way):
        if (half + ring) % 2 == 0:
            return on_section(section_at((place + way) % sections, sections))
        return on_depth((depth + way) % depth_size)

    def send(half, ring, first, second, way, distance):
        part = part_at(distance, way, sizes[half][ring])
        home, row = item(half, first, second)
        place_in = region(home, row, half, part)
        source = own(half, part) if first == 0 and second == 0 else place_in
        at = 0 if way == 1 else 1
        if ring == 0:
            sems = (first_send.at[half, at, distance], first_recv.at[half, at, distance])
        else:
            index = (half, first % sizes[half][0], at, distance)
            sems = (second_send.at[index], second_recv.at[index])
        go(remote(source, place_in, *sems, neighbour(half, ring, way)))

    def receive(half, ring, first, second, way, distance):
        part = part_at(distance, way, sizes[half][ring])
        home, row = item(half, first, second)
        place_in = region(home, row, half, part)
        at = 0 if way == 1 else 1
        if ring == 0:
            sems = (first_send.at[half, at, distance], first_recv.at[half, at, distance])
        else:
            index = (half, first % sizes[half][0], at, distance)
            sems = (second_send.at[index], second_recv.at[index])
        remote(place_in, place_in, *sems, neighbour(half, ring, way)).wait_recv()

    twins = []

    def share(half, first, second):
        home, row = item(half, first, second)
        place_in = region(home, row, half, None)
        source = own(half, None) if first == 0 and second == 0 else place_in
        index = (half, first % sizes[half][0], second % sizes[half][1])
        go(remote(source, place_in, twin_send.at[index], twin_recv.at[index], twin))
        twins.append((half, first, second, index))

    def whole(half, first, second):
        if second == 0:
            for way in (1, -1):
                send(half, 1, first, 0, way, 1)
        share(half, first, second)

    def on_first(half, way, distance):
        size = sizes[half][0]
        receive(half, 0, way * distance, 0, way, distance)
        if (distance + 1) * 2 <= size:
            send(half, 0, way * distance, 0, way, distance + 1)
        if part_at(distance, way, size) is None or way == -1:
            whole(half, way * distance, 0)

    def on_second(half, first, way, distance):
        size = sizes[half][1]
        receive(half, 1, first, way * distance, way, distance)
        if (distance + 1) * 2 <= size:
            send(half, 1, first, way * distance, way, distance + 1)
        if part_at(distance, way, size) is None or way == -1:
            whole(half, first, way * distance)

    events = []
    for half in (0, 1):
        for way, distance, _ in arrivals(sizes[half][0]):
            events.append((distance, 0, half, 0, 0, way, distance))
        firsts = [(0, 0)]
        for way, distance, part in arrivals(sizes[half][0]):
            if part is None or way == -1:
                firsts.append((way * distance, distance))
        for first, ready in firsts:
            for way, distance, _ in arrivals(sizes[half][1]):
                events.append((ready + distance, 1, half, ready, first, way, distance))
    events.sort(key=lambda event: (event[0], event[1], event[3], event[6]))

    for half in (0, 1):
        for way in (1, -1):
            send(half, 0, 0, 0, way, 1)
    for half in (0, 1):
        whole(half, 0, 0)
    for k in range(1, sections):
        other = on_section((section + k) % sections)

        @pl.when(core == 0)
        def _():
            remote(
                down_ref, adapters.at[section, 0], adapter_send.at[k], adapter_recv.at[k], other
            ).start()

        @pl.when(core == 1)
        def _():
            remote(
                up_ref, adapters.at[section, 1], adapter_send.at[k], adapter_recv.at[k], other
            ).start()

    mine = pl.ds(pl.multiple_of(section * rows, rows), rows)
    cameras = camera_ref[mine, :]
    table = camera_table_ref[...].astype(jnp.float32)
    chosen = jnp.zeros((rows, width), jnp.float32)
    for view in range(table.shape[0]):
        chosen = jnp.where(cameras == view, table[view : view + 1, :], chosen)
    camera_rows[...] = chosen
    latent = latent_ref[mine, :].astype(jnp.float32)
    hidden_at[0, 0] = (latent + chosen).astype(jnp.bfloat16)
    step_table = step_table_ref[...].astype(jnp.float32)
    step_rows = lax.broadcasted_iota(jnp.int32, step_table.shape, 0)
    for step in range(2):
        picked = jnp.where(step_rows == steps_ref[step], step_table, 0.0)
        modulation[step] = 1.0 + jnp.sum(picked, axis=0, keepdims=True)

    for _, ring, half, _, first, way, distance in events:
        if ring == 0:
            on_first(half, way, distance)
        else:
            on_second(half, first, way, distance)

    for k in range(1, sections):
        behind = (section - k) % sections
        held = adapters.at[behind, core]
        remote(held, held, adapter_send.at[k], adapter_recv.at[k], on_section(behind)).wait()
        go(remote(held, held, adapter_send.at[sections + k], adapter_recv.at[sections + k], twin))
    for k in range(1, sections):
        behind = (section - k) % sections
        held = adapters.at[behind, 1 - core]
        index = sections + k
        remote(held, held, adapter_send.at[index], adapter_recv.at[index], twin).wait_recv()
    for copy, k in go_gain:
        copy.wait()
    for half, first, second, index in twins:
        home, row = item(half, first, second)
        held = region(home, row, half, None, 1 - core)
        remote(held, held, twin_send.at[index], twin_recv.at[index], twin).wait_recv()
    for copy in local:
        copy.wait()
    for copy in pending:
        copy.wait_send()
    pending.clear()

    def normed_of(step, layer):
        hidden = hidden_at[step, layer].astype(jnp.float32)
        inverse = lax.rsqrt(jnp.mean(hidden * hidden, axis=-1, keepdims=True) + EPSILON)
        gain = gains[layer] * modulation[step]
        return hidden, inverse, gain, (hidden * inverse * gain).astype(jnp.bfloat16)

    def forward(step, layer):
        hidden, _, _, normed = normed_of(step, layer)
        low = lax.dot_general(
            normed, adapters[layer, 0], NT, preferred_element_type=jnp.float32
        ).astype(jnp.bfloat16)
        pre = jnp.dot(
            normed, weights[layer], preferred_element_type=jnp.float32
        ) + ADAPTER_SCALE * jnp.dot(low, adapters[layer, 1], preferred_element_type=jnp.float32)
        pre_at[step, layer] = pre
        low_at[step, layer] = low
        hidden_at[step, layer + 1] = (hidden + jax.nn.silu(pre)).astype(jnp.bfloat16)

    def forward_body(index, carry):
        step, layer = index // sections, index % sections
        forward(step, layer)

        @pl.when((step == 0) & (layer == sections - 1))
        def _():
            last = hidden_at[0, sections].astype(jnp.float32)
            first = latent_ref[mine, :].astype(jnp.float32)
            middle = (BLEND * (first + last)).astype(jnp.bfloat16)
            hidden_at[0, sections] = middle
            hidden_at[1, 0] = (middle.astype(jnp.float32) + camera_rows[...]).astype(jnp.bfloat16)

        return carry

    lax.fori_loop(0, 2 * sections, forward_body, 0)
    final = BLEND * (
        hidden_at[0, sections].astype(jnp.float32) + hidden_at[1, sections].astype(jnp.float32)
    )
    squashed = jnp.tanh(final)
    adjoint = (
        target_ref[mine, :].astype(jnp.float32) * (1.0 - squashed * squashed) * scale_factor
    )
    adjoint_at[...] = adjoint

    def backward(step, layer, gradient, earlier):
        hidden, inverse, gain, normed = normed_of(step, layer)
        pre = pre_at[step, layer]
        sigmoid = jax.nn.sigmoid(pre)
        pre_grad = (gradient * sigmoid * (1.0 + pre * (1.0 - sigmoid))).astype(jnp.bfloat16)
        low_grad = (
            ADAPTER_SCALE
            * lax.dot_general(
                pre_grad, adapters[layer, 1], NT, preferred_element_type=jnp.float32
            )
        ).astype(jnp.bfloat16)
        norm_grad = lax.dot_general(
            pre_grad, weights[layer], NT, preferred_element_type=jnp.float32
        ) + jnp.dot(low_grad, adapters[layer, 0], preferred_element_type=jnp.float32)
        down_term = lax.dot_general(normed, low_grad, TN, preferred_element_type=jnp.float32)
        up_term = ADAPTER_SCALE * lax.dot_general(
            pre_grad, low_at[step, layer], TN, preferred_element_type=jnp.float32
        )
        terms = jnp.concatenate([down_term, up_term], axis=1)
        terms = terms.reshape(depth_size, 2, block, 2 * rank)
        for side in range(2):
            total = terms[:, side]
            if earlier:
                total = total + pair_out[layer, side].astype(jnp.float32)
            pair_out[layer, side] = total.astype(jnp.bfloat16)
        scaled = hidden * inverse
        scaled_grad = norm_grad * gain
        result = gradient + inverse * (
            scaled_grad - scaled * jnp.mean(scaled_grad * scaled, axis=-1, keepdims=True)
        )
        return result.astype(jnp.bfloat16).astype(jnp.float32)

    def to_twin(layer):
        return remote(
            pair_out.at[layer, 1 - core],
            pair_in.at[layer],
            pair_sems.at[0, layer],
            pair_sems.at[1, layer],
            twin,
        )

    def to_depth(layer, k):
        other = (depth + k) % depth_size
        return remote(
            depth_out.at[layer, other],
            depth_in.at[layer, k - 1],
            depth_send.at[layer, k],
            depth_recv.at[layer, k],
            on_depth(other),
        )

    def pass_on(layer):
        to_twin(layer).wait_recv()
        total = pair_out[layer, core].astype(jnp.float32) + pair_in[layer].astype(jnp.float32)
        depth_out[layer] = total.astype(jnp.bfloat16)
        for k in range(1, depth_size):
            to_depth(layer, k).start()

    def late_body(index, gradient):
        layer = sections - 1 - index
        gradient = backward(1, layer, gradient, False)
        return gradient

    def early_body(index, gradient):
        layer = sections - 1 - index
        gradient = backward(0, layer, gradient, True)
        to_twin(layer).start()

        @pl.when(index > 0)
        def _():
            pass_on(layer + 1)

        return gradient

    gradient = lax.fori_loop(0, sections, late_body, BLEND * adjoint)
    gradient = BLEND * (BLEND * adjoint_at[...] + gradient)
    lax.fori_loop(0, sections, early_body, gradient)
    pass_on(0)

    def settle(layer, carry):
        total = depth_out[layer, depth].astype(jnp.float32)
        for k in range(1, depth_size):
            to_depth(layer, k).wait()
            total = total + depth_in[layer, k - 1].astype(jnp.float32)
        plane_out[layer] = total.astype(jnp.bfloat16)
        to_twin(layer).wait_send()
        return carry

    lax.fori_loop(0, sections, settle, 0)
    copies = []
    for k in range(1, sections):
        other = (section + k) % sections
        copy = remote(
            plane_out.at[other],
            plane_in.at[k - 1],
            plane_send.at[k],
            plane_recv.at[k],
            on_section(other),
        )
        copy.start()
        copies.append(copy)
    total = plane_out[section].astype(jnp.float32)
    for k, copy in enumerate(copies):
        copy.wait()
        total = total + plane_in[k].astype(jnp.float32)
    out_ref[...] = total


def local(
    latent,
    target,
    camera_of_token,
    timestep_indices,
    camera_embedding_table,
    timestep_embedding_table,
    layer_norm_gain,
    frozen_weight,
    adapter_down_weight,
    adapter_up_weight,
):
    sections, ways = lax.axis_size("section"), lax.axis_size("dp")
    width = latent.shape[1]
    rank = adapter_down_weight.shape[1]
    block = frozen_weight.shape[1]
    rows = latent.shape[0] // sections
    depth_size = ways // 2
    scale_factor = 1.0 / math.sqrt(latent.shape[0] * ways)
    longest = max(sections, depth_size)
    dma = pltpu.SemaphoreType.DMA
    bf16, f32 = jnp.bfloat16, jnp.float32
    vmem = pl.BlockSpec(memory_space=pltpu.VMEM)
    result = pl.pallas_call(
        functools.partial(kernel, sections, ways, scale_factor),
        out_shape=jax.ShapeDtypeStruct((block, 2 * rank), f32),
        in_specs=[pl.BlockSpec(memory_space=pltpu.SMEM)] + [vmem] * 9,
        out_specs=vmem,
        scratch_shapes=[
            pltpu.VMEM((sections, width, width), bf16),
            pltpu.VMEM((sections, 2, rank, width), bf16),
            pltpu.VMEM((sections, 1, width), f32),
            pltpu.VMEM((2, sections + 1, rows, width), bf16),
            pltpu.VMEM((2, sections, rows, width), f32),
            pltpu.VMEM((2, sections, rows, rank), bf16),
            pltpu.VMEM((2, 1, width), f32),
            pltpu.VMEM((rows, width), f32),
            pltpu.VMEM((rows, width), f32),
            pltpu.VMEM((sections, 2, depth_size, block, 2 * rank), bf16),
            pltpu.VMEM((sections, depth_size, block, 2 * rank), bf16),
            pltpu.VMEM((sections, depth_size, block, 2 * rank), bf16),
            pltpu.VMEM((sections, depth_size - 1, block, 2 * rank), bf16),
            pltpu.VMEM((sections, block, 2 * rank), bf16),
            pltpu.VMEM((sections - 1, block, 2 * rank), bf16),
            dma((4,)),
            dma((2, 2, longest // 2 + 1)),
            dma((2, 2, longest // 2 + 1)),
            dma((2, longest, 2, longest // 2 + 1)),
            dma((2, longest, 2, longest // 2 + 1)),
            dma((2, longest, longest)),
            dma((2, longest, longest)),
            dma((sections,)),
            dma((sections,)),
            dma((2 * sections,)),
            dma((2 * sections,)),
            dma((2, sections)),
            dma((sections, depth_size)),
            dma((sections, depth_size)),
            dma((sections,)),
            dma((sections,)),
        ],
        compiler_params=pltpu.CompilerParams(
            collective_id=0, has_side_effects=True, vmem_limit_bytes=66 * 1024 * 1024 - 2 * 1024 * 1024 - 65536
        ),
    )(
        timestep_indices,
        latent,
        target,
        camera_of_token[:, None],
        camera_embedding_table,
        timestep_embedding_table,
        layer_norm_gain,
        frozen_weight[0],
        adapter_down_weight[0],
        adapter_up_weight[0],
    )
    turned = result.T
    return (turned[None, :rank], turned[None, rank:])


def solution(mesh):
    in_specs = (
        P("dp", None),
        P("dp", None),
        P("dp"),
        P(),
        P(),
        P(),
        P("section", None),
        P("section", "dp", None),
        P("section", None, None),
        P("section", None, None),
    )
    out_specs = (P("section", None, "dp"), P("section", None, "dp"))
    return jax.shard_map(local, mesh=mesh, in_specs=in_specs, out_specs=out_specs, check_vma=False)
```

```python
import functools
import math

import jax
import jax.numpy as jnp
from jax import lax
from jax.experimental import pallas as pl
from jax.experimental.pallas import tpu as pltpu
from jax.sharding import PartitionSpec as P

BLEND = 0.5
ADAPTER_SCALE = 0.5
EPSILON = 1e-06
MESH = pl.DeviceIdType.MESH
NT = (((1,), (1,)), ((), ()))
TN = (((0,), (0,)), ((), ()))


def bits_of(size):
    bits = size.bit_length() - 1
    return bits if 2**bits == size else 0


def section_at(place, size):
    bits = bits_of(size)
    if not bits:
        return place
    bit = [(place // 2**i) % 2 for i in range(bits)] + [0]
    return sum(((bit[i] + bit[i + 1]) % 2) * 2**i for i in range(bits))


def place_of(section, size):
    bits = bits_of(size)
    if not bits:
        return section
    upper, place = 0, 0
    for i in reversed(range(bits)):
        upper = ((section // 2**i) % 2 + upper) % 2
        place = place + upper * 2**i
    return place


def arrivals(size):
    half = size // 2
    steps = []
    for distance in range(1, half + 1):
        for way in (1, -1):
            if distance < half or size % 2:
                steps.append((way, distance, None))
            else:
                steps.append((way, distance, 0 if way == 1 else 1))
    return steps


def part_at(distance, way, size):
    if distance < size // 2 or size % 2:
        return None
    return 0 if way == 1 else 1


def kernel(
    sections,
    ways,
    scale_factor,
    steps_ref,
    latent_ref,
    target_ref,
    camera_ref,
    camera_table_ref,
    step_table_ref,
    gain_ref,
    shard_ref,
    down_ref,
    up_ref,
    down_out_ref,
    up_out_ref,
    weights,
    adapters,
    gains,
    hidden_at,
    pre_at,
    low_at,
    modulation,
    camera_rows,
    adjoint_at,
    pair_out,
    pair_in,
    depth_out,
    depth_in,
    plane_out,
    plane_in,
    local_sem,
    first_send,
    first_recv,
    second_send,
    second_recv,
    twin_send,
    twin_recv,
    small_send,
    small_recv,
    adapter_send,
    adapter_recv,
    pair_sems,
    depth_send,
    depth_recv,
    plane_send,
    plane_recv,
):
    section, lane = lax.axis_index("section"), lax.axis_index("dp")
    depth_size = ways // 2
    depth, core = lane // 2, lane % 2
    place = place_of(section, sections)
    block, width = shard_ref.shape
    rows = hidden_at.shape[2]
    rank = down_ref.shape[0]
    twin = (section, depth * 2 + 1 - core)

    def on_section(other):
        return (other, lane)

    def on_depth(other):
        return (section, other * 2 + core)

    barrier = pltpu.get_barrier_semaphore()
    friends = [twin]
    friends += [on_section((section + k) % sections) for k in range(1, sections)]
    friends += [on_depth((depth + k) % depth_size) for k in range(1, depth_size)]
    for friend in friends:
        pl.semaphore_signal(barrier, inc=1, device_id=friend, device_id_type=MESH)
    pl.semaphore_wait(barrier, len(friends))

    def remote(source, target, send, recv, device):
        return pltpu.make_async_remote_copy(
            src_ref=source,
            dst_ref=target,
            send_sem=send,
            recv_sem=recv,
            device_id=device,
            device_id_type=MESH,
        )

    pending = []

    def go(copy):
        copy.start()
        pending.append(copy)

    go_gain, go_adapter = [], []
    for k in range(1, sections):
        other = on_section((section + k) % sections)
        copy = remote(gain_ref, gains.at[section], small_send.at[k], small_recv.at[k], other)
        copy.start()
        go_gain.append((copy, k))

    tiles = width // 128
    cut = max(tiles // 4, 1)

    def columns_of(half, part):
        start, stop = (0, cut) if half == 0 else (cut, tiles)
        middle = (start + stop) // 2
        if part is not None:
            start, stop = (start, middle) if part == 0 else (middle, stop)
        return pl.ds(start * 128, (stop - start) * 128)

    def region(home, row, half, part, side=core):
        offset = pl.multiple_of((row * 2 + side) * block, block)
        return weights.at[home, pl.ds(offset, block), columns_of(half, part)]

    def own(half, part):
        return shard_ref.at[:, columns_of(half, part)]

    local = [
        pltpu.make_async_copy(
            shard_ref,
            weights.at[section, pl.ds(pl.multiple_of(lane * block, block), block), :],
            local_sem.at[0],
        ),
        pltpu.make_async_copy(gain_ref, gains.at[section], local_sem.at[1]),
        pltpu.make_async_copy(down_ref, adapters.at[section, 0], local_sem.at[2]),
        pltpu.make_async_copy(up_ref, adapters.at[section, 1], local_sem.at[3]),
    ]
    for copy in local:
        copy.start()

    sizes = ((sections, depth_size), (depth_size, sections))
    spots = ((place, depth), (depth, place))

    def item(half, first, second):
        at_first = (spots[half][0] - first) % sizes[half][0]
        at_second = (spots[half][1] - second) % sizes[half][1]
        if half == 0:
            return section_at(at_first, sections), at_second
        return section_at(at_second, sections), at_first

    def neighbour(half, ring, way):
        if (half + ring) % 2 == 0:
            return on_section(section_at((place + way) % sections, sections))
        return on_depth((depth + way) % depth_size)

    def send(half, ring, first, second, way, distance):
        part = part_at(distance, way, sizes[half][ring])
        home, row = item(half, first, second)
        place_in = region(home, row, half, part)
        source = own(half, part) if first == 0 and second == 0 else place_in
        at = 0 if way == 1 else 1
        if ring == 0:
            sems = (first_send.at[half, at, distance], first_recv.at[half, at, distance])
        else:
            index = (half, first % sizes[half][0], at, distance)
            sems = (second_send.at[index], second_recv.at[index])
        go(remote(source, place_in, *sems, neighbour(half, ring, way)))

    def receive(half, ring, first, second, way, distance):
        part = part_at(distance, way, sizes[half][ring])
        home, row = item(half, first, second)
        place_in = region(home, row, half, part)
        at = 0 if way == 1 else 1
        if ring == 0:
            sems = (first_send.at[half, at, distance], first_recv.at[half, at, distance])
        else:
            index = (half, first % sizes[half][0], at, distance)
            sems = (second_send.at[index], second_recv.at[index])
        remote(place_in, place_in, *sems, neighbour(half, ring, way)).wait_recv()

    twins = []

    def share(half, first, second):
        home, row = item(half, first, second)
        place_in = region(home, row, half, None)
        source = own(half, None) if first == 0 and second == 0 else place_in
        index = (half, first % sizes[half][0], second % sizes[half][1])
        go(remote(source, place_in, twin_send.at[index], twin_recv.at[index], twin))
        twins.append((half, first, second, index))

    def whole(half, first, second):
        if second == 0:
            for way in (1, -1):
                send(half, 1, first, 0, way, 1)
        share(half, first, second)

    def on_first(half, way, distance):
        size = sizes[half][0]
        receive(half, 0, way * distance, 0, way, distance)
        if (distance + 1) * 2 <= size:
            send(half, 0, way * distance, 0, way, distance + 1)
        if part_at(distance, way, size) is None or way == -1:
            whole(half, way * distance, 0)

    def on_second(half, first, way, distance):
        size = sizes[half][1]
        receive(half, 1, first, way * distance, way, distance)
        if (distance + 1) * 2 <= size:
            send(half, 1, first, way * distance, way, distance + 1)
        if part_at(distance, way, size) is None or way == -1:
            whole(half, first, way * distance)

    events = []
    for half in (0, 1):
        for way, distance, _ in arrivals(sizes[half][0]):
            events.append((distance, 0, half, 0, 0, way, distance))
        firsts = [(0, 0)]
        for way, distance, part in arrivals(sizes[half][0]):
            if part is None or way == -1:
                firsts.append((way * distance, distance))
        for first, ready in firsts:
            for way, distance, _ in arrivals(sizes[half][1]):
                events.append((ready + distance, 1, half, ready, first, way, distance))
    events.sort(key=lambda event: (event[0], event[1], event[3], event[6]))

    for half in (0, 1):
        for way in (1, -1):
            send(half, 0, 0, 0, way, 1)
    for half in (0, 1):
        whole(half, 0, 0)
    for k in range(1, sections):
        other = on_section((section + k) % sections)

        @pl.when(core == 0)
        def _():
            remote(
                down_ref, adapters.at[section, 0], adapter_send.at[k], adapter_recv.at[k], other
            ).start()

        @pl.when(core == 1)
        def _():
            remote(
                up_ref, adapters.at[section, 1], adapter_send.at[k], adapter_recv.at[k], other
            ).start()

    mine = pl.ds(pl.multiple_of(section * rows, rows), rows)
    cameras = camera_ref[mine, :]
    table = camera_table_ref[...].astype(jnp.float32)
    chosen = jnp.zeros((rows, width), jnp.float32)
    for view in range(table.shape[0]):
        chosen = jnp.where(cameras == view, table[view : view + 1, :], chosen)
    camera_rows[...] = chosen
    latent = latent_ref[mine, :].astype(jnp.float32)
    hidden_at[0, 0] = (latent + chosen).astype(jnp.bfloat16)
    step_table = step_table_ref[...].astype(jnp.float32)
    step_rows = lax.broadcasted_iota(jnp.int32, step_table.shape, 0)
    for step in range(2):
        picked = jnp.where(step_rows == steps_ref[step], step_table, 0.0)
        modulation[step] = 1.0 + jnp.sum(picked, axis=0, keepdims=True)

    def hand_adapters():
        for k in range(1, sections):
            behind = (section - k) % sections
            held = adapters.at[behind, core]
            remote(held, held, adapter_send.at[k], adapter_recv.at[k], on_section(behind)).wait()
            go(remote(held, held, adapter_send.at[sections + k], adapter_recv.at[sections + k], twin))

    handed = False
    for level, ring, half, _, first, way, distance in events:
        if level > 1 and not handed:
            hand_adapters()
            handed = True
        if ring == 0:
            on_first(half, way, distance)
        else:
            on_second(half, first, way, distance)

    for k in range(1, sections):
        behind = (section - k) % sections
        held = adapters.at[behind, 1 - core]
        index = sections + k
        remote(held, held, adapter_send.at[index], adapter_recv.at[index], twin).wait_recv()
    for copy, k in go_gain:
        copy.wait()
    for half, first, second, index in twins:
        home, row = item(half, first, second)
        held = region(home, row, half, None, 1 - core)
        remote(held, held, twin_send.at[index], twin_recv.at[index], twin).wait_recv()
    for copy in local:
        copy.wait()

    def normed_of(step, layer):
        hidden = hidden_at[step, layer].astype(jnp.float32)
        inverse = lax.rsqrt(jnp.mean(hidden * hidden, axis=-1, keepdims=True) + EPSILON)
        gain = gains[layer] * modulation[step]
        return hidden, inverse, gain, (hidden * inverse * gain).astype(jnp.bfloat16)

    def forward(step, layer):
        hidden, _, _, normed = normed_of(step, layer)
        low = lax.dot_general(
            normed, adapters[layer, 0], NT, preferred_element_type=jnp.float32
        ).astype(jnp.bfloat16)
        pre = jnp.dot(
            normed, weights[layer], preferred_element_type=jnp.float32
        ) + ADAPTER_SCALE * jnp.dot(low, adapters[layer, 1], preferred_element_type=jnp.float32)
        pre_at[step, layer] = pre
        low_at[step, layer] = low
        hidden_at[step, layer + 1] = (hidden + jax.nn.silu(pre)).astype(jnp.bfloat16)

    def forward_body(index, carry):
        step, layer = index // sections, index % sections
        forward(step, layer)

        @pl.when((step == 0) & (layer == sections - 1))
        def _():
            last = hidden_at[0, sections].astype(jnp.float32)
            first = latent_ref[mine, :].astype(jnp.float32)
            middle = (BLEND * (first + last)).astype(jnp.bfloat16)
            hidden_at[0, sections] = middle
            hidden_at[1, 0] = (middle.astype(jnp.float32) + camera_rows[...]).astype(jnp.bfloat16)

        return carry

    lax.fori_loop(0, 2 * sections, forward_body, 0)
    final = BLEND * (
        hidden_at[0, sections].astype(jnp.float32) + hidden_at[1, sections].astype(jnp.float32)
    )
    squashed = jnp.tanh(final)
    adjoint = (
        target_ref[mine, :].astype(jnp.float32) * (1.0 - squashed * squashed) * scale_factor
    )
    adjoint_at[...] = adjoint

    def backward(step, layer, gradient, earlier):
        hidden, inverse, gain, normed = normed_of(step, layer)
        pre = pre_at[step, layer]
        sigmoid = jax.nn.sigmoid(pre)
        pre_grad = (gradient * sigmoid * (1.0 + pre * (1.0 - sigmoid))).astype(jnp.bfloat16)
        low_grad = (
            ADAPTER_SCALE
            * lax.dot_general(
                pre_grad, adapters[layer, 1], NT, preferred_element_type=jnp.float32
            )
        ).astype(jnp.bfloat16)
        norm_grad = lax.dot_general(
            pre_grad, weights[layer], NT, preferred_element_type=jnp.float32
        ) + jnp.dot(low_grad, adapters[layer, 0], preferred_element_type=jnp.float32)
        down_term = lax.dot_general(normed, low_grad, TN, preferred_element_type=jnp.float32)
        up_term = ADAPTER_SCALE * lax.dot_general(
            pre_grad, low_at[step, layer], TN, preferred_element_type=jnp.float32
        )
        terms = jnp.concatenate([down_term, up_term], axis=1)
        terms = terms.reshape(depth_size, 2, block, 2 * rank)
        for side in range(2):
            total = terms[:, side]
            if earlier:
                total = total + pair_out[layer, side].astype(jnp.float32)
            pair_out[layer, side] = total.astype(jnp.bfloat16)
        scaled = hidden * inverse
        scaled_grad = norm_grad * gain
        result = gradient + inverse * (
            scaled_grad - scaled * jnp.mean(scaled_grad * scaled, axis=-1, keepdims=True)
        )
        return result.astype(jnp.bfloat16).astype(jnp.float32)

    def to_twin(layer):
        return remote(
            pair_out.at[layer, 1 - core],
            pair_in.at[layer],
            pair_sems.at[0, layer],
            pair_sems.at[1, layer],
            twin,
        )

    def to_depth(layer, k):
        other = (depth + k) % depth_size
        return remote(
            depth_out.at[layer, other],
            depth_in.at[layer, k - 1],
            depth_send.at[layer, k],
            depth_recv.at[layer, k],
            on_depth(other),
        )

    def pass_on(layer):
        to_twin(layer).wait_recv()
        total = pair_out[layer, core].astype(jnp.float32) + pair_in[layer].astype(jnp.float32)
        depth_out[layer] = total.astype(jnp.bfloat16)
        for k in range(1, depth_size):
            to_depth(layer, k).start()

    def late_body(index, gradient):
        layer = sections - 1 - index
        gradient = backward(1, layer, gradient, False)
        return gradient

    def early_body(index, gradient):
        layer = sections - 1 - index
        gradient = backward(0, layer, gradient, True)
        to_twin(layer).start()

        @pl.when(index > 0)
        def _():
            pass_on(layer + 1)

        return gradient

    gradient = lax.fori_loop(0, sections, late_body, BLEND * adjoint)
    gradient = BLEND * (BLEND * adjoint_at[...] + gradient)
    lax.fori_loop(0, sections, early_body, gradient)
    pass_on(0)

    def to_section(layer):
        k = (layer - section) % sections
        return remote(
            plane_out.at[layer],
            plane_in.at[k - 1],
            plane_send.at[k],
            plane_recv.at[k],
            on_section(layer),
        )

    def settle(index, carry):
        layer = sections - 1 - index
        total = depth_out[layer, depth].astype(jnp.float32)
        for k in range(1, depth_size):
            to_depth(layer, k).wait()
            total = total + depth_in[layer, k - 1].astype(jnp.float32)
        plane_out[layer] = total.astype(jnp.bfloat16)

        @pl.when(layer != section)
        def _():
            to_section(layer).start()

        to_twin(layer).wait_send()
        return carry

    lax.fori_loop(0, sections, settle, 0)
    total = plane_out[section].astype(jnp.float32)
    for k in range(1, sections):
        to_section((section + k) % sections).wait()
        total = total + plane_in[k - 1].astype(jnp.float32)
    for copy in pending:
        copy.wait_send()
    turned = total.T
    down_out_ref[...] = turned[:rank]
    up_out_ref[...] = turned[rank:]


def local(
    latent,
    target,
    camera_of_token,
    timestep_indices,
    camera_embedding_table,
    timestep_embedding_table,
    layer_norm_gain,
    frozen_weight,
    adapter_down_weight,
    adapter_up_weight,
):
    sections, ways = lax.axis_size("section"), lax.axis_size("dp")
    width = latent.shape[1]
    rank = adapter_down_weight.shape[1]
    block = frozen_weight.shape[1]
    rows = latent.shape[0] // sections
    depth_size = ways // 2
    scale_factor = 1.0 / math.sqrt(latent.shape[0] * ways)
    longest = max(sections, depth_size)
    dma = pltpu.SemaphoreType.DMA
    bf16, f32 = jnp.bfloat16, jnp.float32
    vmem = pl.BlockSpec(memory_space=pltpu.VMEM)
    result = pl.pallas_call(
        functools.partial(kernel, sections, ways, scale_factor),
        out_shape=[jax.ShapeDtypeStruct((rank, block), f32)] * 2,
        in_specs=[pl.BlockSpec(memory_space=pltpu.SMEM)] + [vmem] * 9,
        out_specs=[vmem] * 2,
        scratch_shapes=[
            pltpu.VMEM((sections, width, width), bf16),
            pltpu.VMEM((sections, 2, rank, width), bf16),
            pltpu.VMEM((sections, 1, width), f32),
            pltpu.VMEM((2, sections + 1, rows, width), bf16),
            pltpu.VMEM((2, sections, rows, width), f32),
            pltpu.VMEM((2, sections, rows, rank), bf16),
            pltpu.VMEM((2, 1, width), f32),
            pltpu.VMEM((rows, width), f32),
            pltpu.VMEM((rows, width), f32),
            pltpu.VMEM((sections, 2, depth_size, block, 2 * rank), bf16),
            pltpu.VMEM((sections, depth_size, block, 2 * rank), bf16),
            pltpu.VMEM((sections, depth_size, block, 2 * rank), bf16),
            pltpu.VMEM((sections, depth_size - 1, block, 2 * rank), bf16),
            pltpu.VMEM((sections, block, 2 * rank), bf16),
            pltpu.VMEM((sections - 1, block, 2 * rank), bf16),
            dma((4,)),
            dma((2, 2, longest // 2 + 1)),
            dma((2, 2, longest // 2 + 1)),
            dma((2, longest, 2, longest // 2 + 1)),
            dma((2, longest, 2, longest // 2 + 1)),
            dma((2, longest, longest)),
            dma((2, longest, longest)),
            dma((sections,)),
            dma((sections,)),
            dma((2 * sections,)),
            dma((2 * sections,)),
            dma((2, sections)),
            dma((sections, depth_size)),
            dma((sections, depth_size)),
            dma((sections,)),
            dma((sections,)),
        ],
        compiler_params=pltpu.CompilerParams(
            collective_id=0, has_side_effects=True, vmem_limit_bytes=66 * 1024 * 1024 - 2 * 1024 * 1024 - 65536
        ),
    )(
        timestep_indices,
        latent,
        target,
        camera_of_token[:, None],
        camera_embedding_table,
        timestep_embedding_table,
        layer_norm_gain,
        frozen_weight[0],
        adapter_down_weight[0],
        adapter_up_weight[0],
    )
    return (result[0][None], result[1][None])


def solution(mesh):
    in_specs = (
        P("dp", None),
        P("dp", None),
        P("dp"),
        P(),
        P(),
        P(),
        P("section", None),
        P("section", "dp", None),
        P("section", None, None),
        P("section", None, None),
    )
    out_specs = (P("section", None, "dp"), P("section", None, "dp"))
    return jax.shard_map(local, mesh=mesh, in_specs=in_specs, out_specs=out_specs, check_vma=False)
```
